32 devices in a mesh: parts: 2 (over x), grid: 8 (over z, y), depth: 2 (over core).
Axes of the slice: x: 2, y: 2, z: 4, core: 2. Of those that a mesh axis runs over, the one named last changes fastest.
Arguments:
- gate_input: bfloat16 [1024, 32768], P(('parts', 'depth'), 'grid'), parts along dimension 0, may hold values from -6 to 6
- up_input: bfloat16 [1024, 32768], P(('parts', 'depth'), 'grid'), parts along dimension 0, may hold values from -6 to 6
- code_values: bfloat16 [32768, 8192], P('grid', 'depth'), may hold values from -6 to 6, as said below
- exponents: int32 [1024, 8192], P('grid', 'depth'), may hold values from -10 to -7
- cotangent: bfloat16 [1024, 8192], P(('parts', 'depth'), 'grid'), parts along dimension 0, may hold values from -1.5 to 1.5
Outputs:
- output_rows: bfloat16 [1024, 8192], P(('parts', 'depth'), 'grid'), parts along dimension 0
- grad_gate: bfloat16 [1024, 32768], P(('parts', 'depth'), 'grid'), parts along dimension 0
- grad_up: bfloat16 [1024, 32768], P(('parts', 'depth'), 'grid'), parts along dimension 0
- grad_weight: bfloat16 [65536, 8192], P(('parts', 'grid'), 'depth'), parts along dimension 0
The draws below stay inside these ranges and needn't reach their ends.
There are 2 independent parts, one for each index of `parts`. The reference program is written for one: setup_inputs(seed, part) draws one part's arguments, and reference() takes and returns one part's arrays. A program takes and returns all parts, laid end to end along the dimension named above; an argument that names none is the same for every part. Nothing has to cross between parts.
Inputs may be any that keep to these rules, and one draw needn't show every extreme that they name: `code_values`: every entry is one of the E2M1 values 0, +-0.5, +-1, +-1.5, +-2, +-3, +-4, +-6.
All inputs are finite; a program needn't handle non-finite values.
Results may differ from the reference program's by a relative error of at most 0.0049.
Values may be sent and summed in bfloat16 or wider, within the bound.
A program may use at most 448 MiB of HBM per device.

```python
import jax
import jax.numpy as jnp

D = 8192
FFW = 32768
BLOCK = 32
TOKENS = 512


def draw_code_values(key, part):
    table = jnp.array([0.0, 0.5, 1.0, 1.5, 2.0, 3.0, 4.0, 6.0, 0.0, -0.5, -1.0, -1.5, -2.0, -3.0, -4.0, -6.0], jnp.float32)
    codes = jax.random.randint(jax.random.fold_in(key, 11), (FFW, D), 0, 16)
    return jnp.take(table, codes).astype(jnp.bfloat16)


def set_ends(values, rng, least, largest):
    spot = [jax.random.randint(jax.random.fold_in(rng, axis), (), 0, length) for axis, length in enumerate(values.shape)]
    widest = values.shape.index(max(values.shape))
    beside = spot[:widest] + [(spot[widest] + 1) % values.shape[widest]] + spot[widest + 1:]
    return values.at[tuple(spot)].set(least).at[tuple(beside)].set(largest)


def steps_of(rng, dims, cuts, least, largest):
    def one(dim, parts):
        heights = jax.random.uniform(jax.random.fold_in(jax.random.fold_in(rng, 6), dim), (parts,), jnp.float32, least / len(cuts), largest / len(cuts))
        return jnp.repeat(jnp.exp(heights), dims[dim] // parts).reshape((-1,) + (1,) * (len(dims) - dim - 1))

    gain = one(*cuts[0])
    for cut in cuts[1:]:
        gain = gain * one(*cut)
    return gain


def scatter_about(key, extent, deviation, bound, shards=(), kind=jnp.bfloat16):
    result = deviation * jax.random.normal(key, extent, jnp.float32)
    if shards:
        result = result * steps_of(key, extent, shards, -0.22, 0.18)
    return jnp.clip(result, -bound, bound).astype(kind)


def setup_inputs(seed: int = 0, part: int = 0) -> dict:
    splits = jax.random.split(jax.random.key(seed), 6)
    part_keys = jax.random.split(jax.random.fold_in(splits[5], part), 6)
    gate_input = scatter_about(part_keys[0], (TOKENS, FFW), 1.0, 6.0, ((0, 2), (1, 8)))
    up_input = scatter_about(part_keys[1], (TOKENS, FFW), 1.0, 6.0, ((0, 2), (1, 8)))
    code_values = draw_code_values(jax.random.fold_in(splits[5], 71), part)
    exponents = set_ends(jax.random.randint(splits[3], (FFW // BLOCK, D), -10, -6), jax.random.fold_in(splits[3], 1), -10, (-6) - 1).astype(jnp.int32)
    cotangent = scatter_about(part_keys[4], (TOKENS, D), 0.25, 1.5, ((0, 2), (1, 8)))
    return {"gate_input": gate_input, "up_input": up_input, "code_values": code_values, "exponents": exponents, "cotangent": cotangent}


def dequantize(code_values, exponents):
    scaled = jnp.exp2(exponents.astype(jnp.float32))
    blocks = code_values.astype(jnp.float32).reshape(FFW // BLOCK, BLOCK, D) * scaled[:, None, :]
    return blocks.reshape(FFW, D).astype(jnp.bfloat16)


def reference(gate_input, up_input, code_values, exponents, cotangent):
    weight = dequantize(code_values, exponents)
    gate_float = gate_input.astype(jnp.float32)
    up_float = up_input.astype(jnp.float32)
    sigmoid_gate = jax.nn.sigmoid(gate_float)
    activated = gate_float * sigmoid_gate
    hidden = (activated * up_float).astype(jnp.bfloat16)
    output_rows = jnp.dot(hidden, weight, preferred_element_type=jnp.float32).astype(jnp.bfloat16)
    grad_hidden = jnp.dot(cotangent, weight.T, preferred_element_type=jnp.float32)
    slope = sigmoid_gate * (1.0 + gate_float * (1.0 - sigmoid_gate))
    grad_gate = (grad_hidden * up_float * slope).astype(jnp.bfloat16)
    grad_up = (grad_hidden * activated).astype(jnp.bfloat16)
    grad_weight = jnp.dot(hidden.T, cotangent, preferred_element_type=jnp.float32).astype(jnp.bfloat16)
    return (output_rows, grad_gate, grad_up, grad_weight)
```

```python
import functools

import jax
import jax.numpy as jnp
from jax import lax
from jax.experimental import pallas as pl
from jax.experimental.pallas import tpu as pltpu
from jax.sharding import PartitionSpec as P

VMEM_LIMIT = 60 * 1024 * 1024
F32, BF16 = jnp.float32, jnp.bfloat16


def tile(size, most):
    width = min(size, most)
    while size % width:
        width //= 2
    return width


def dequantized(codes, exponents):
    rows, columns = codes.shape
    scale = jnp.exp2(exponents.astype(F32)).astype(BF16)
    return (codes.reshape(rows // 32, 32, columns) * scale[:, None, :]).reshape(rows, columns)


def forward_body(depth, mine_ref, other_ref, codes_ref, exponents_ref, out_mine_ref, out_other_ref):
    units = codes_ref.shape[0]
    totals = [None, None]
    for start in range(0, units, depth):
        weight = dequantized(
            codes_ref[start : start + depth, :], exponents_ref[start // 32 : (start + depth) // 32, :]
        )
        for index, ref in enumerate((mine_ref, other_ref)):
            term = jnp.dot(ref[:, start : start + depth], weight, preferred_element_type=F32)
            totals[index] = term if totals[index] is None else totals[index] + term
    out_mine_ref[...] = totals[0].astype(out_mine_ref.dtype)
    out_other_ref[...] = totals[1].astype(out_other_ref.dtype)


def forward(mine, other, codes, exponents, dtype):
    tokens, units = mine.shape
    columns = codes.shape[1]
    width = tile(columns, 512)
    whole = pl.BlockSpec((tokens, units), lambda j: (0, 0), pipeline_mode=pl.Buffered(1))
    return pl.pallas_call(
        functools.partial(forward_body, tile(units, 1024)),
        grid=(columns // width,),
        in_specs=[
            whole,
            whole,
            pl.BlockSpec((units, width), lambda j: (0, j)),
            pl.BlockSpec((units // 32, width), lambda j: (0, j)),
        ],
        out_specs=[pl.BlockSpec((tokens, width), lambda j: (0, j))] * 2,
        out_shape=[jax.ShapeDtypeStruct((tokens, columns), dtype)] * 2,
        compiler_params=pltpu.CompilerParams(vmem_limit_bytes=VMEM_LIMIT),
        cost_estimate=pl.CostEstimate(
            flops=4 * tokens * units * columns, bytes_accessed=2 * units * columns, transcendentals=0
        ),
        name="forward",
    )(mine, other, codes, exponents)


def hidden_grad_body(depth, mine_ref, other_ref, codes_ref, exponents_ref, grad_mine_ref, grad_other_ref):
    columns = codes_ref.shape[1]
    totals = [None, None]
    for start in range(0, columns, depth):
        weight = dequantized(codes_ref[:, start : start + depth], exponents_ref[:, start : start + depth])
        for index, ref in enumerate((mine_ref, other_ref)):
            term = lax.dot_general(
                ref[:, start : start + depth], weight, (((1,), (1,)), ((), ())), preferred_element_type=F32
            )
            totals[index] = term if totals[index] is None else totals[index] + term
    grad_mine_ref[...] = totals[0].astype(grad_mine_ref.dtype)
    grad_other_ref[...] = totals[1].astype(grad_other_ref.dtype)


def hidden_grad(mine, other, codes, exponents):
    tokens, columns = mine.shape
    units = codes.shape[0]
    height = tile(units, 512)
    whole = pl.BlockSpec((tokens, columns), lambda i: (0, 0), pipeline_mode=pl.Buffered(1))
    return pl.pallas_call(
        functools.partial(hidden_grad_body, tile(columns, 1024)),
        grid=(units // height,),
        in_specs=[
            whole,
            whole,
            pl.BlockSpec((height, columns), lambda i: (i, 0)),
            pl.BlockSpec((height // 32, columns), lambda i: (i, 0)),
        ],
        out_specs=[pl.BlockSpec((tokens, height), lambda i: (0, i))] * 2,
        out_shape=[jax.ShapeDtypeStruct((tokens, units), F32), jax.ShapeDtypeStruct((tokens, units), BF16)],
        compiler_params=pltpu.CompilerParams(vmem_limit_bytes=VMEM_LIMIT),
        cost_estimate=pl.CostEstimate(
            flops=4 * tokens * units * columns, bytes_accessed=2 * units * columns, transcendentals=0
        ),
        name="hidden_grad",
    )(mine, other, codes, exponents)


def weight_grad_body(width, h_mine_ref, h_other_ref, c_mine_ref, c_other_ref, out_ref):
    left = [h_mine_ref[...].T, h_other_ref[...].T]
    for start in range(0, out_ref.shape[1], width):
        total = None
        for rows, ref in zip(left, (c_mine_ref, c_other_ref)):
            term = jnp.dot(rows, ref[:, start : start + width], preferred_element_type=F32)
            total = term if total is None else total + term
        out_ref[:, start : start + width] = total.astype(out_ref.dtype)


def weight_grad(h_mine, h_other, c_mine, c_other):
    tokens, units = h_mine.shape
    columns = c_mine.shape[1]
    height = tile(units, 512)
    whole = pl.BlockSpec((tokens, columns), lambda i: (0, 0), pipeline_mode=pl.Buffered(1))
    part = pl.BlockSpec((tokens, height), lambda i: (0, i))
    return pl.pallas_call(
        functools.partial(weight_grad_body, tile(columns, 1024)),
        grid=(units // height,),
        in_specs=[part, part, whole, whole],
        out_specs=pl.BlockSpec((height, columns), lambda i: (i, 0)),
        out_shape=jax.ShapeDtypeStruct((units, columns), BF16),
        compiler_params=pltpu.CompilerParams(vmem_limit_bytes=VMEM_LIMIT),
        cost_estimate=pl.CostEstimate(
            flops=4 * tokens * units * columns, bytes_accessed=2 * units * columns, transcendentals=0
        ),
        name="weight_grad",
    )(h_mine, h_other, c_mine, c_other)


def shards(gate_input, up_input, code_values, exponents, cotangent):
    core = lax.axis_index("depth")
    half = code_values.shape[1]

    def swap(value):
        return lax.ppermute(value, "depth", [(0, 1), (1, 0)])

    cotangent_all = lax.all_gather(cotangent, "grid", axis=1, tiled=True)
    gate_float = gate_input.astype(F32)
    up_float = up_input.astype(F32)
    sigmoid_gate = jax.nn.sigmoid(gate_float)
    activated = gate_float * sigmoid_gate
    hidden = (activated * up_float).astype(BF16)
    hidden_other = swap(hidden)
    out_mine, out_other = forward(hidden, hidden_other, code_values, exponents, BF16)
    out_came = swap(out_other)
    low = jnp.where(core == 0, out_mine, out_came)
    high = jnp.where(core == 0, out_came, out_mine)
    share = jnp.concatenate([low, high], axis=1).astype(F32)
    output_rows = lax.psum_scatter(share, "grid", scatter_dimension=1, tiled=True).astype(BF16)

    low, high = cotangent_all[:, :half], cotangent_all[:, half:]
    cot_mine = jnp.where(core == 0, low, high)
    cot_other = swap(jnp.where(core == 0, high, low))
    grad_mine, grad_other = hidden_grad(cot_mine, cot_other, code_values, exponents)
    grad_came = swap(grad_other)
    grad_weight = weight_grad(hidden, hidden_other, cot_mine, cot_other)
    grad_hidden = grad_mine + grad_came.astype(F32)
    slope = sigmoid_gate * (1.0 + gate_float * (1.0 - sigmoid_gate))
    grad_gate = (grad_hidden * up_float * slope).astype(BF16)
    grad_up = (grad_hidden * activated).astype(BF16)
    return (output_rows, grad_gate, grad_up, grad_weight)


def solution(mesh):
    tokens_units = P(("parts", "depth"), "grid")
    weights = P("grid", "depth")
    return jax.shard_map(
        shards,
        mesh=mesh,
        in_specs=(tokens_units, tokens_units, weights, weights, tokens_units),
        out_specs=(tokens_units, tokens_units, tokens_units, P(("parts", "grid"), "depth")),
        check_vma=False,
    )
```

```python
import functools

import jax
import jax.numpy as jnp
from jax import lax
from jax.experimental import pallas as pl
from jax.experimental.pallas import tpu as pltpu
from jax.sharding import PartitionSpec as P

VMEM_LIMIT = 60 * 1024 * 1024
F32, BF16 = jnp.float32, jnp.bfloat16


MESH = pl.DeviceIdType.MESH


def line_sizes(count):
    fast = 1
    while 4 * fast * fast <= count:
        fast *= 2
    return count // fast, fast


def position(fast):
    me = lax.axis_index("grid")
    return me, me // fast, me % fast, lax.axis_index("depth")


def greet(slow, fast):
    me, row, column, core = position(fast)
    barrier = pltpu.get_barrier_semaphore()

    def hail(grid, depth):
        pl.semaphore_signal(barrier, inc=1, device_id={"grid": grid, "depth": depth}, device_id_type=MESH)

    for step in range(1, slow):
        hail((row + step) % slow * fast + column, core)
    for step in range(1, fast):
        for depth in range(2):
            hail(row * fast + (column + step) % fast, depth)
    hail(me, 1 - core)
    pl.semaphore_wait(barrier, slow - 1 + 2 * (fast - 1) + 1)


def remote(source, target, send, recv, grid, depth):
    return pltpu.make_async_remote_copy(
        src_ref=source,
        dst_ref=target,
        send_sem=send,
        recv_sem=recv,
        device_id={"grid": grid, "depth": depth},
        device_id_type=MESH,
    )


def tile(size, most):
    width = min(size, most)
    while size % width:
        width //= 2
    return width


def dequantized(codes, exponents):
    rows, columns = codes.shape
    scale = jnp.exp2(exponents.astype(F32)).astype(BF16)
    return (codes.reshape(rows // 32, 32, columns) * scale[:, None, :]).reshape(rows, columns)


def forward_body(
    depth,
    slow,
    fast,
    mine_ref,
    other_ref,
    codes_ref,
    exponents_ref,
    cot_ref,
    out_mine_ref,
    out_other_ref,
    all_ref,
    own_sem,
    line_sem,
    relay_sem,
    recv_sem,
):
    step = pl.program_id(0)
    last = pl.num_programs(0) - 1
    me, row, column, core = position(fast)
    width = cot_ref.shape[1]
    near = slow // 2

    def away(source_row):
        gap = source_row // near - core
        return gap * gap

    def piece(section, source_row, source_column):
        index = source_row % near * fast + source_column
        place = all_ref.at[section, :, pl.ds(pl.multiple_of(index * width, width), width)]
        return place, recv_sem.at[section, index]

    own_place, own_recv = piece(2 * away(row), row, column)

    def keep_own():
        return pltpu.make_async_copy(cot_ref, own_place, own_sem)

    def along(hop):
        return remote(
            cot_ref, own_place, line_sem.at[hop], own_recv, (row + hop) % slow * fast + column, core
        )

    def across(hop, turn):
        source_row = (row + hop) % slow
        source = cot_ref if hop == 0 else piece(2 * away(source_row), source_row, column)[0]
        place, recv = piece(away(source_row), source_row, column)
        target = row * fast + (column + turn) % fast
        return remote(source, place, relay_sem.at[hop, turn], recv, target, source_row // near)

    def relay(hop, finish):
        def one(turn):
            copy = across(hop, turn)
            if finish:
                copy.wait_send()
            else:
                copy.start()

        for turn in range(1, fast):
            one(turn)

        @pl.when(away((row + hop) % slow) == 1)
        def _():
            one(0)

    def arrive(section, source_row, source_column):
        place, recv = piece(section, source_row, source_column)
        pltpu.make_async_copy(place, place, recv).wait()

    @pl.when(step == 0)
    def _():
        greet(slow, fast)
        for hop in range(1, slow):
            along(hop).start()
        relay(0, False)

        @pl.when(away(row) == 0)
        def _():
            keep_own().start()

    units = codes_ref.shape[0]
    totals = [None, None]
    for start in range(0, units, depth):
        weight = dequantized(
            codes_ref[start : start + depth, :], exponents_ref[start // 32 : (start + depth) // 32, :]
        )
        for index, ref in enumerate((mine_ref, other_ref)):
            term = jnp.dot(ref[:, start : start + depth], weight, preferred_element_type=F32)
            totals[index] = term if totals[index] is None else totals[index] + term
    out_mine_ref[...] = totals[0].astype(out_mine_ref.dtype)
    out_other_ref[...] = totals[1].astype(out_other_ref.dtype)

    for count, hop in enumerate(range(1, slow)):

        @pl.when(step == jnp.minimum(last, (count + 1) * (last + 1) // (slow - 1)))
        def _():
            source_row = (row + hop) % slow
            arrive(2 * away(source_row), source_row, column)
            relay(hop, False)

    @pl.when(step == last)
    def _():
        for index in range(near):
            for turn in range(1, fast):
                arrive(0, core * near + index, (column + turn) % fast)
            for source_column in range(fast):
                arrive(1, core * near + index, source_column)
        for hop in range(1, slow):
            along(hop).wait_send()
        for hop in range(slow):
            relay(hop, True)

        @pl.when(away(row) == 0)
        def _():
            keep_own().wait()


def forward(mine, other, codes, exponents, cotangent, slow, fast):
    tokens, units = mine.shape
    columns = codes.shape[1]
    width = tile(columns, 512)
    whole = pl.BlockSpec((tokens, units), lambda j: (0, 0), pipeline_mode=pl.Buffered(1))
    anywhere = pl.BlockSpec(memory_space=pl.ANY)
    dma = pltpu.SemaphoreType.DMA
    return pl.pallas_call(
        functools.partial(forward_body, tile(units, 1024), slow, fast),
        grid=(columns // width,),
        in_specs=[
            whole,
            whole,
            pl.BlockSpec((units, width), lambda j: (0, j)),
            pl.BlockSpec((units // 32, width), lambda j: (0, j)),
            anywhere,
        ],
        out_specs=[pl.BlockSpec((tokens, width), lambda j: (0, j))] * 2 + [anywhere],
        out_shape=[jax.ShapeDtypeStruct((tokens, columns), BF16)] * 2
        + [jax.ShapeDtypeStruct((3, tokens, columns), BF16)],
        scratch_shapes=[dma, dma((slow,)), dma((slow, fast)), dma((3, slow * fast // 2))],
        compiler_params=pltpu.CompilerParams(
            vmem_limit_bytes=VMEM_LIMIT, collective_id=0, has_side_effects=True
        ),
        cost_estimate=pl.CostEstimate(
            flops=4 * tokens * units * columns, bytes_accessed=2 * units * columns, transcendentals=0
        ),
        name="forward",
    )(mine, other, codes, exponents, cotangent)


def hidden_grad_body(
    depth,
    slow,
    fast,
    mine_ref,
    other_ref,
    codes_ref,
    exponents_ref,
    out_mine_ref,
    out_other_ref,
    grad_mine_ref,
    grad_other_ref,
    rows_ref,
    first_ref,
    sums_ref,
    second_ref,
    first_send,
    first_recv,
    second_send,
    second_recv,
):
    step = pl.program_id(0)
    last = pl.num_programs(0) - 1
    me, row, column, core = position(fast)
    width = rows_ref.shape[1]
    near = slow // 2

    def block(ref, index, turn):
        start = (index * fast + (column + turn) % fast) * width
        return ref.at[:, pl.ds(pl.multiple_of(start, width), width)]

    def keep_own(index):
        target_row = core * near + index
        return pltpu.make_async_copy(
            block(out_mine_ref, index, 0), first_ref.at[target_row, column], first_recv.at[target_row, column]
        )

    def across(index, turn, other):
        target_row = core * near + index
        return remote(
            block(out_other_ref if other else out_mine_ref, index, turn),
            first_ref.at[target_row, column],
            first_send.at[index, turn, other],
            first_recv.at[target_row, column],
            row * fast + (column + turn) % fast,
            1 - core if other else core,
        )

    def crossings():
        return [
            (index, turn, other)
            for index in range(near)
            for turn in [*range(1, fast), 0]
            for other in range(2)
            if turn or other
        ]

    def gathered(target_row):
        total = None
        for source in range(fast):
            place = first_ref.at[target_row, source]
            pltpu.make_async_copy(place, place, first_recv.at[target_row, source]).wait()
            term = first_ref[target_row, source].astype(F32)
            total = term if total is None else total + term
        return total

    def along(hop):
        target_row = (row + hop) % slow
        return remote(
            sums_ref.at[hop],
            second_ref.at[row],
            second_send.at[hop],
            second_recv.at[row],
            target_row * fast + column,
            core,
        )

    @pl.when(step == 0)
    def _():
        greet(slow, fast)
        for crossing in crossings():
            across(*crossing).start()
        for index in range(near):
            keep_own(index).start()

    columns = codes_ref.shape[1]
    totals = [None, None]
    for start in range(0, columns, depth):
        weight = dequantized(codes_ref[:, start : start + depth], exponents_ref[:, start : start + depth])
        for index, ref in enumerate((mine_ref, other_ref)):
            term = lax.dot_general(
                ref[:, start : start + depth], weight, (((1,), (1,)), ((), ())), preferred_element_type=F32
            )
            totals[index] = term if totals[index] is None else totals[index] + term
    grad_mine_ref[...] = totals[0].astype(grad_mine_ref.dtype)
    grad_other_ref[...] = totals[1].astype(grad_other_ref.dtype)

    for hop in range(1, slow):

        @pl.when(step == jnp.minimum(last, hop * (last + 1) // (slow - 1)))
        def _():
            sums_ref[hop] = gathered((row + hop) % slow).astype(BF16)
            along(hop).start()

    @pl.when(step == last)
    def _():
        total = gathered(row)
        for hop in range(1, slow):
            source = (row + hop) % slow
            place = second_ref.at[source]
            pltpu.make_async_copy(place, place, second_recv.at[source]).wait()
            total = total + second_ref[source].astype(F32)
        rows_ref[...] = total.astype(rows_ref.dtype)
        for crossing in crossings():
            across(*crossing).wait_send()
        for hop in range(1, slow):
            along(hop).wait_send()


def hidden_grad(cot_all, codes, exponents, out_mine, out_other, slow, fast):
    _, tokens, columns = cot_all.shape
    units = codes.shape[0]
    height = tile(units, 512)
    width = columns * 2 // (slow * fast)
    anywhere = pl.BlockSpec(memory_space=pl.ANY)
    dma = pltpu.SemaphoreType.DMA
    return pl.pallas_call(
        functools.partial(hidden_grad_body, tile(columns, 1024), slow, fast),
        grid=(units // height,),
        in_specs=[
            pl.BlockSpec((None, tokens, columns), lambda i: (0, 0, 0), pipeline_mode=pl.Buffered(1)),
            pl.BlockSpec((None, tokens, columns), lambda i: (1, 0, 0), pipeline_mode=pl.Buffered(1)),
            pl.BlockSpec((height, columns), lambda i: (i, 0)),
            pl.BlockSpec((height // 32, columns), lambda i: (i, 0)),
            anywhere,
            anywhere,
        ],
        out_specs=[pl.BlockSpec((tokens, height), lambda i: (0, i))] * 2
        + [pl.BlockSpec((tokens, width), lambda i: (0, 0))],
        out_shape=[
            jax.ShapeDtypeStruct((tokens, units), F32),
            jax.ShapeDtypeStruct((tokens, units), BF16),
            jax.ShapeDtypeStruct((tokens, width), BF16),
        ],
        scratch_shapes=[
            pltpu.VMEM((slow, fast, tokens, width), BF16),
            pltpu.VMEM((slow, tokens, width), BF16),
            pltpu.VMEM((slow, tokens, width), BF16),
            dma((slow // 2, fast, 2)),
            dma((slow, fast)),
            dma((slow,)),
            dma((slow,)),
        ],
        compiler_params=pltpu.CompilerParams(
            vmem_limit_bytes=VMEM_LIMIT, collective_id=1, has_side_effects=True
        ),
        cost_estimate=pl.CostEstimate(
            flops=4 * tokens * units * columns, bytes_accessed=2 * units * columns, transcendentals=0
        ),
        name="hidden_grad",
    )(cot_all, cot_all, codes, exponents, out_mine, out_other)


def weight_grad_body(width, h_mine_ref, h_other_ref, c_mine_ref, c_other_ref, out_ref):
    left = [h_mine_ref[...].T, h_other_ref[...].T]
    for start in range(0, out_ref.shape[1], width):
        total = None
        for rows, ref in zip(left, (c_mine_ref, c_other_ref)):
            term = jnp.dot(rows, ref[:, start : start + width], preferred_element_type=F32)
            total = term if total is None else total + term
        out_ref[:, start : start + width] = total.astype(out_ref.dtype)


def weight_grad(h_mine, h_other, cot_all):
    tokens, units = h_mine.shape
    columns = cot_all.shape[2]
    height = tile(units, 512)
    first = pl.BlockSpec((None, tokens, columns), lambda i: (0, 0, 0), pipeline_mode=pl.Buffered(1))
    second = pl.BlockSpec((None, tokens, columns), lambda i: (1, 0, 0), pipeline_mode=pl.Buffered(1))
    part = pl.BlockSpec((tokens, height), lambda i: (0, i))
    return pl.pallas_call(
        functools.partial(weight_grad_body, tile(columns, 1024)),
        grid=(units // height,),
        in_specs=[part, part, first, second],
        out_specs=pl.BlockSpec((height, columns), lambda i: (i, 0)),
        out_shape=jax.ShapeDtypeStruct((units, columns), BF16),
        compiler_params=pltpu.CompilerParams(vmem_limit_bytes=VMEM_LIMIT),
        cost_estimate=pl.CostEstimate(
            flops=4 * tokens * units * columns, bytes_accessed=2 * units * columns, transcendentals=0
        ),
        name="weight_grad",
    )(h_mine, h_other, cot_all, cot_all)


def shards(slow, fast, gate_input, up_input, code_values, exponents, cotangent):
    def swap(value):
        return lax.ppermute(value, "depth", [(0, 1), (1, 0)])

    gate_float = gate_input.astype(F32)
    up_float = up_input.astype(F32)
    sigmoid_gate = jax.nn.sigmoid(gate_float)
    activated = gate_float * sigmoid_gate
    hidden = (activated * up_float).astype(BF16)
    hidden_other = swap(hidden)
    out_mine, out_other, cot_all = forward(
        hidden, hidden_other, code_values, exponents, cotangent, slow, fast
    )
    grad_mine, grad_other, output_rows = hidden_grad(
        cot_all, code_values, exponents, out_mine, out_other, slow, fast
    )
    grad_came = swap(grad_other)
    grad_weight = weight_grad(hidden, hidden_other, cot_all)
    grad_hidden = grad_mine + grad_came.astype(F32)
    slope = sigmoid_gate * (1.0 + gate_float * (1.0 - sigmoid_gate))
    grad_gate = (grad_hidden * up_float * slope).astype(BF16)
    grad_up = (grad_hidden * activated).astype(BF16)
    return (output_rows, grad_gate, grad_up, grad_weight)


def solution(mesh):
    tokens_units = P(("parts", "depth"), "grid")
    weights = P("grid", "depth")
    slow, fast = line_sizes(mesh.shape["grid"])
    return jax.shard_map(
        functools.partial(shards, slow, fast),
        mesh=mesh,
        in_specs=(tokens_units, tokens_units, weights, weights, tokens_units),
        out_specs=(tokens_units, tokens_units, tokens_units, P(("parts", "grid"), "depth")),
        check_vma=False,
    )
```

```python
import functools

import jax
import jax.numpy as jnp
from jax import lax
from jax.experimental import pallas as pl
from jax.experimental.pallas import tpu as pltpu
from jax.sharding import PartitionSpec as P

VMEM_LIMIT = 60 * 1024 * 1024
F32, BF16 = jnp.float32, jnp.bfloat16


MESH = pl.DeviceIdType.MESH


def line_sizes(count):
    fast = 1
    while 4 * fast * fast <= count:
        fast *= 2
    return count // fast, fast


def position(fast):
    me = lax.axis_index("grid")
    return me, me // fast, me % fast, lax.axis_index("depth")


def greet(slow, fast):
    me, row, column, core = position(fast)
    barrier = pltpu.get_barrier_semaphore()

    def hail(grid, depth):
        pl.semaphore_signal(barrier, inc=1, device_id={"grid": grid, "depth": depth}, device_id_type=MESH)

    for step in range(1, slow):
        hail((row + step) % slow * fast + column, core)
    for step in range(1, fast):
        for depth in range(2):
            hail(row * fast + (column + step) % fast, depth)
    hail(me, 1 - core)
    pl.semaphore_wait(barrier, slow - 1 + 2 * (fast - 1) + 1)


def remote(source, target, send, recv, grid, depth):
    return pltpu.make_async_remote_copy(
        src_ref=source,
        dst_ref=target,
        send_sem=send,
        recv_sem=recv,
        device_id={"grid": grid, "depth": depth},
        device_id_type=MESH,
    )


def tile(size, most):
    width = min(size, most)
    while size % width:
        width //= 2
    return width


def dequantized(codes, exponents):
    rows, columns = codes.shape
    scale = jnp.exp2(exponents.astype(F32)).astype(BF16)
    return (codes.reshape(rows // 32, 32, columns) * scale[:, None, :]).reshape(rows, columns)


def forward_body(
    depth,
    slow,
    fast,
    mine_ref,
    other_ref,
    codes_ref,
    exponents_ref,
    cot_ref,
    out_mine_ref,
    out_other_ref,
    all_ref,
    own_sem,
    line_sem,
    relay_sem,
    recv_sem,
):
    step = pl.program_id(0)
    last = pl.num_programs(0) - 1
    me, row, column, core = position(fast)
    width = cot_ref.shape[1]
    near = slow // 2

    def away(source_row):
        gap = source_row // near - core
        return gap * gap

    def piece(section, source_row, source_column):
        index = source_row % near * fast + source_column
        place = all_ref.at[section, :, pl.ds(pl.multiple_of(index * width, width), width)]
        return place, recv_sem.at[section, index]

    order = sorted(range(1, slow), key=lambda hop: hop * (slow - hop))
    own_place, own_recv = piece(2 * away(row), row, column)

    def keep_own():
        return pltpu.make_async_copy(cot_ref, own_place, own_sem)

    def along(hop):
        return remote(
            cot_ref, own_place, line_sem.at[hop], own_recv, (row + hop) % slow * fast + column, core
        )

    def across(hop, turn):
        source_row = (row + hop) % slow
        source = cot_ref if hop == 0 else piece(2 * away(source_row), source_row, column)[0]
        place, recv = piece(away(source_row), source_row, column)
        target = row * fast + (column + turn) % fast
        return remote(source, place, relay_sem.at[hop, turn], recv, target, source_row // near)

    def relay(hop, finish):
        def one(turn):
            copy = across(hop, turn)
            if finish:
                copy.wait_send()
            else:
                copy.start()

        for turn in range(1, fast):
            one(turn)

        @pl.when(away((row + hop) % slow) == 1)
        def _():
            one(0)

    def arrive(section, source_row, source_column):
        place, recv = piece(section, source_row, source_column)
        pltpu.make_async_copy(place, place, recv).wait()

    @pl.when(step == 0)
    def _():
        greet(slow, fast)
        along(order[0]).start()
        relay(0, False)

        @pl.when(away(row) == 0)
        def _():
            keep_own().start()

    units = codes_ref.shape[0]
    totals = [None, None]
    for start in range(0, units, depth):
        weight = dequantized(
            codes_ref[start : start + depth, :], exponents_ref[start // 32 : (start + depth) // 32, :]
        )
        for index, ref in enumerate((mine_ref, other_ref)):
            term = jnp.dot(ref[:, start : start + depth], weight, preferred_element_type=F32)
            totals[index] = term if totals[index] is None else totals[index] + term
    out_mine_ref[...] = totals[0].astype(out_mine_ref.dtype)
    out_other_ref[...] = totals[1].astype(out_other_ref.dtype)

    for count, hop in enumerate(slow - hop for hop in order):

        @pl.when(step == jnp.minimum(last, (count + 1) * (last + 1) // (slow - 1)))
        def _():
            source_row = (row + hop) % slow
            arrive(2 * away(source_row), source_row, column)
            if count + 1 < len(order):
                along(order[count + 1]).start()
            relay(hop, False)

    @pl.when(step == last)
    def _():
        for index in range(near):
            for turn in range(1, fast):
                arrive(0, core * near + index, (column + turn) % fast)
            for source_column in range(fast):
                arrive(1, core * near + index, source_column)
        for hop in range(1, slow):
            along(hop).wait_send()
        for hop in range(slow):
            relay(hop, True)

        @pl.when(away(row) == 0)
        def _():
            keep_own().wait()


def forward(mine, other, codes, exponents, cotangent, slow, fast):
    tokens, units = mine.shape
    columns = codes.shape[1]
    width = tile(columns, 512)
    whole = pl.BlockSpec((tokens, units), lambda j: (0, 0), pipeline_mode=pl.Buffered(1))
    anywhere = pl.BlockSpec(memory_space=pl.ANY)
    dma = pltpu.SemaphoreType.DMA
    return pl.pallas_call(
        functools.partial(forward_body, tile(units, 1024), slow, fast),
        grid=(columns // width,),
        in_specs=[
            whole,
            whole,
            pl.BlockSpec((units, width), lambda j: (0, j)),
            pl.BlockSpec((units // 32, width), lambda j: (0, j)),
            anywhere,
        ],
        out_specs=[pl.BlockSpec((tokens, width), lambda j: (0, j))] * 2 + [anywhere],
        out_shape=[jax.ShapeDtypeStruct((tokens, columns), BF16)] * 2
        + [jax.ShapeDtypeStruct((3, tokens, columns), BF16)],
        scratch_shapes=[dma, dma((slow,)), dma((slow, fast)), dma((3, slow * fast // 2))],
        compiler_params=pltpu.CompilerParams(
            vmem_limit_bytes=VMEM_LIMIT, collective_id=0, has_side_effects=True
        ),
        cost_estimate=pl.CostEstimate(
            flops=4 * tokens * units * columns, bytes_accessed=2 * units * columns, transcendentals=0
        ),
        name="forward",
    )(mine, other, codes, exponents, cotangent)


def hidden_grad_body(
    depth,
    slow,
    fast,
    mine_ref,
    other_ref,
    codes_ref,
    exponents_ref,
    out_mine_ref,
    out_other_ref,
    grad_mine_ref,
    grad_other_ref,
    rows_ref,
    first_ref,
    sums_ref,
    second_ref,
    first_send,
    first_recv,
    second_send,
    second_recv,
):
    step = pl.program_id(0)
    last = pl.num_programs(0) - 1
    me, row, column, core = position(fast)
    width = rows_ref.shape[1]
    near = slow // 2

    def block(ref, index, turn):
        start = (index * fast + (column + turn) % fast) * width
        return ref.at[:, pl.ds(pl.multiple_of(start, width), width)]

    def keep_own(index):
        target_row = core * near + index
        return pltpu.make_async_copy(
            block(out_mine_ref, index, 0), first_ref.at[target_row, column], first_recv.at[target_row, column]
        )

    def across(index, turn, other):
        target_row = core * near + index
        return remote(
            block(out_other_ref if other else out_mine_ref, index, turn),
            first_ref.at[target_row, column],
            first_send.at[index, turn, other],
            first_recv.at[target_row, column],
            row * fast + (column + turn) % fast,
            1 - core if other else core,
        )

    def crossings(wave):
        index = (row + 1 + wave) % near
        turns = [*range(1, fast), 0]
        return [across(index, turn, other) for turn in turns for other in range(2) if turn or other]

    def launch(wave):
        for copy in crossings(wave):
            copy.start()
        keep_own((row + 1 + wave) % near).start()

    def targets(wave):
        index = (row + 1 + wave) % near
        distant = (row // near + 1) % 2 * near + index
        return [distant] if wave == near - 1 else [distant, row // near * near + index]

    def gathered(target_row):
        total = None
        for source in range(fast):
            place = first_ref.at[target_row, source]
            pltpu.make_async_copy(place, place, first_recv.at[target_row, source]).wait()
            term = first_ref[target_row, source].astype(F32)
            total = term if total is None else total + term
        return total

    def along(target_row):
        return remote(
            sums_ref.at[target_row],
            second_ref.at[row],
            second_send.at[target_row],
            second_recv.at[row],
            target_row * fast + column,
            core,
        )

    @pl.when(step == 0)
    def _():
        greet(slow, fast)
        launch(0)

    columns = codes_ref.shape[1]
    totals = [None, None]
    for start in range(0, columns, depth):
        weight = dequantized(codes_ref[:, start : start + depth], exponents_ref[:, start : start + depth])
        for index, ref in enumerate((mine_ref, other_ref)):
            term = lax.dot_general(
                ref[:, start : start + depth], weight, (((1,), (1,)), ((), ())), preferred_element_type=F32
            )
            totals[index] = term if totals[index] is None else totals[index] + term
    grad_mine_ref[...] = totals[0].astype(grad_mine_ref.dtype)
    grad_other_ref[...] = totals[1].astype(grad_other_ref.dtype)

    for wave in range(near):

        @pl.when(step == jnp.minimum(last, (wave + 1) * (last + 1) // (near + 1)))
        def _():
            for count, target_row in enumerate(targets(wave)):
                total = gathered(target_row)
                sums_ref[target_row] = total.astype(BF16)
                along(target_row).start()
                if count == 0 and wave + 1 < near:
                    launch(wave + 1)

    @pl.when(step == last)
    def _():
        total = gathered(row)
        for hop in range(1, slow):
            source = (row + hop) % slow
            place = second_ref.at[source]
            pltpu.make_async_copy(place, place, second_recv.at[source]).wait()
            total = total + second_ref[source].astype(F32)
        rows_ref[...] = total.astype(rows_ref.dtype)
        for wave in range(near):
            for copy in crossings(wave):
                copy.wait_send()
            for target_row in targets(wave):
                along(target_row).wait_send()


def hidden_grad(cot_all, codes, exponents, out_mine, out_other, slow, fast):
    _, tokens, columns = cot_all.shape
    units = codes.shape[0]
    height = tile(units, 512)
    width = columns * 2 // (slow * fast)
    anywhere = pl.BlockSpec(memory_space=pl.ANY)
    dma = pltpu.SemaphoreType.DMA
    return pl.pallas_call(
        functools.partial(hidden_grad_body, tile(columns, 1024), slow, fast),
        grid=(units // height,),
        in_specs=[
            pl.BlockSpec((None, tokens, columns), lambda i: (0, 0, 0), pipeline_mode=pl.Buffered(1)),
            pl.BlockSpec((None, tokens, columns), lambda i: (1, 0, 0), pipeline_mode=pl.Buffered(1)),
            pl.BlockSpec((height, columns), lambda i: (i, 0)),
            pl.BlockSpec((height // 32, columns), lambda i: (i, 0)),
            anywhere,
            anywhere,
        ],
        out_specs=[pl.BlockSpec((tokens, height), lambda i: (0, i))] * 2
        + [pl.BlockSpec((tokens, width), lambda i: (0, 0))],
        out_shape=[
            jax.ShapeDtypeStruct((tokens, units), F32),
            jax.ShapeDtypeStruct((tokens, units), BF16),
            jax.ShapeDtypeStruct((tokens, width), BF16),
        ],
        scratch_shapes=[
            pltpu.VMEM((slow, fast, tokens, width), BF16),
            pltpu.VMEM((slow, tokens, width), BF16),
            pltpu.VMEM((slow, tokens, width), BF16),
            dma((slow // 2, fast, 2)),
            dma((slow, fast)),
            dma((slow,)),
            dma((slow,)),
        ],
        compiler_params=pltpu.CompilerParams(
            vmem_limit_bytes=VMEM_LIMIT, collective_id=1, has_side_effects=True
        ),
        cost_estimate=pl.CostEstimate(
            flops=4 * tokens * units * columns, bytes_accessed=2 * units * columns, transcendentals=0
        ),
        name="hidden_grad",
    )(cot_all, cot_all, codes, exponents, out_mine, out_other)


def weight_grad_body(width, h_mine_ref, h_other_ref, c_mine_ref, c_other_ref, out_ref):
    left = [h_mine_ref[...].T, h_other_ref[...].T]
    for start in range(0, out_ref.shape[1], width):
        total = None
        for rows, ref in zip(left, (c_mine_ref, c_other_ref)):
            term = jnp.dot(rows, ref[:, start : start + width], preferred_element_type=F32)
            total = term if total is None else total + term
        out_ref[:, start : start + width] = total.astype(out_ref.dtype)


def weight_grad(h_mine, h_other, cot_all):
    tokens, units = h_mine.shape
    columns = cot_all.shape[2]
    height = tile(units, 512)
    first = pl.BlockSpec((None, tokens, columns), lambda i: (0, 0, 0), pipeline_mode=pl.Buffered(1))
    second = pl.BlockSpec((None, tokens, columns), lambda i: (1, 0, 0), pipeline_mode=pl.Buffered(1))
    part = pl.BlockSpec((tokens, height), lambda i: (0, i))
    return pl.pallas_call(
        functools.partial(weight_grad_body, tile(columns, 1024)),
        grid=(units // height,),
        in_specs=[part, part, first, second],
        out_specs=pl.BlockSpec((height, columns), lambda i: (i, 0)),
        out_shape=jax.ShapeDtypeStruct((units, columns), BF16),
        compiler_params=pltpu.CompilerParams(vmem_limit_bytes=VMEM_LIMIT),
        cost_estimate=pl.CostEstimate(
            flops=4 * tokens * units * columns, bytes_accessed=2 * units * columns, transcendentals=0
        ),
        name="weight_grad",
    )(h_mine, h_other, cot_all, cot_all)


def shards(slow, fast, gate_input, up_input, code_values, exponents, cotangent):
    def swap(value):
        return lax.ppermute(value, "depth", [(0, 1), (1, 0)])

    gate_float = gate_input.astype(F32)
    up_float = up_input.astype(F32)
    sigmoid_gate = jax.nn.sigmoid(gate_float)
    activated = gate_float * sigmoid_gate
    hidden = (activated * up_float).astype(BF16)
    hidden_other = swap(hidden)
    out_mine, out_other, cot_all = forward(
        hidden, hidden_other, code_values, exponents, cotangent, slow, fast
    )
    grad_mine, grad_other, output_rows = hidden_grad(
        cot_all, code_values, exponents, out_mine, out_other, slow, fast
    )
    grad_came = swap(grad_other)
    grad_weight = weight_grad(hidden, hidden_other, cot_all)
    grad_hidden = grad_mine + grad_came.astype(F32)
    slope = sigmoid_gate * (1.0 + gate_float * (1.0 - sigmoid_gate))
    grad_gate = (grad_hidden * up_float * slope).astype(BF16)
    grad_up = (grad_hidden * activated).astype(BF16)
    return (output_rows, grad_gate, grad_up, grad_weight)


def solution(mesh):
    tokens_units = P(("parts", "depth"), "grid")
    weights = P("grid", "depth")
    slow, fast = line_sizes(mesh.shape["grid"])
    return jax.shard_map(
        functools.partial(shards, slow, fast),
        mesh=mesh,
        in_specs=(tokens_units, tokens_units, weights, weights, tokens_units),
        out_specs=(tokens_units, tokens_units, tokens_units, P(("parts", "grid"), "depth")),
        check_vma=False,
    )
```
